32 devices in a mesh: seq: 2 (over y), exp: 8 (over z, x), enc: 2 (over core).
Axes of the slice: x: 2, y: 2, z: 4, core: 2. Of those that a mesh axis runs over, the one named last changes fastest.
Arguments:
- patches: bfloat16 [8, 4, 272, 1152], P('exp', ('seq', 'enc')), may hold values from -6 to 6
- image_counts: int32 [8, 4], P('exp'), may hold values from 1 to 68, 256 in all within a row
- image_order: int32 [8, 4], P('exp'), may hold values from 0 to 3, each once within a row
- w_merge: bfloat16 [4608, 3456], P(None, ('seq', 'enc')), may hold values from -0.09375 to 0.09375
- w_proj_out: bfloat16 [2, 2, 864, 7168], P(None, 'enc', None, 'seq'), may hold values from -0.109375 to 0.109375
- routes: int32 [2048, 8], P(('exp', 'enc')), may hold values from 0 to 383, all different within a row; in each aligned block of 128 rows (0 to 127, 128 to 255, ...) at most 3 rows name the same one
- route_weight: float32 [2048, 8], P(('exp', 'enc')), may hold values from 0.2 to 1
- expert_place: int32 [384], replicated, may hold values from -1 to 7, as said below
- w_gate: bfloat16 [8, 7168, 1024], P('exp', None, 'seq'), may hold values from -0.0625 to 0.0625
- w_up: bfloat16 [8, 7168, 1024], P('exp', None, 'seq'), may hold values from -0.0625 to 0.0625
- w_down: bfloat16 [8, 1024, 7168], P('exp', 'seq'), may hold values from -0.1875 to 0.1875
Outputs:
- hidden_out: bfloat16 [2048, 7168], P(('exp', 'enc'), 'seq')
- expert_load: float32 [8, 2], P('exp', 'enc')
The draws below stay inside these ranges and needn't reach their ends.
Inputs may be any that keep to these rules, and one draw needn't show every extreme that they name: `image_counts`: in each row the counts sum to 256 and the largest is exactly 68. `image_order`: each row is a permutation of 0 to 3. `routes`: each row names 8 different experts; among the 128 rows of one device no expert is named by more than 3 rows, a bound that some block reaches. `expert_place`: each of 0 to 7 appears exactly once; every other entry is -1.
All inputs are finite; a program needn't handle non-finite values.
Results may differ from the reference program's by a relative error of at most 0.014.
Values may be sent and summed in bfloat16 or wider, within the bound.
A program may use at most 128 MiB of HBM per device.

```python
import math
from functools import partial
import jax
import jax.numpy as jnp
import numpy as np
from jax import lax

D = 7168
VIT = 1152
ALL_EXPERTS = 384
TOP = 8
MERGE = 4
PROJ_H = 3456
EXP_H = 1024
CAP = 3
TOK_DEV = 128
SHARDS = 4
SEQ_TOK = 256
IMG_CAP = 68
TOKENS = 2048
EXPERTS = 8
N_SEQ = 2
N_EXP = 8
N_ENC = 2


def draw_expert_place(key, part):
    shuffled = jax.random.permutation(jax.random.fold_in(key, 7), ALL_EXPERTS)
    numbers = jnp.arange(ALL_EXPERTS, dtype=jnp.int32)
    holder = jnp.where(numbers < EXPERTS, numbers, -1).astype(jnp.int32)
    return jnp.zeros((ALL_EXPERTS,), jnp.int32).at[shuffled].set(holder)


def levels(own_key, shape, cuts, low, largest):
    factor_of, own = 1.0, jax.random.fold_in(own_key, 6)
    for dim, parts in cuts:
        heights = jnp.exp(jax.random.uniform(jax.random.fold_in(own, dim), (parts,), jnp.float32, low / len(cuts), largest / len(cuts)))
        factor_of = factor_of * jnp.repeat(heights, shape[dim] // parts).reshape([-1 if axis == dim else 1 for axis in range(len(shape))])
    return factor_of


def length_profile(amount, total, reach, slope):
    loads = [(1 << 20) // math.isqrt(rank ** slope) + 1 for rank in range(2, amount + 1)]
    spare, given = total - reach - (amount - 1), [1] * (amount - 1)
    while spare > 0:
        free = [i for i in range(amount - 1) if given[i] < reach]
        whole, remaining = sum([loads[i] for i in free]), spare
        for i in free:
            addition = min(reach - given[i], max(1, remaining * loads[i] // whole), spare)
            given[i] = given[i] + addition
            spare = spare - addition
    return np.array([reach] + given)


def ragged(rng, count, total, limit, skew):
    if count == 2:
        one = jax.random.randint(rng, (), max(1, total - limit), min(limit, total - 1) + 1)
        return jnp.stack([one, total - one])
    tallies = jnp.asarray(length_profile(count, total, limit, skew), jnp.int32)
    twos = (count - 1) // 2
    donor, sink = tallies[1:1 + 2 * twos:2], tallies[2:2 + 2 * twos:2]
    room = jnp.minimum(donor - 1, limit - sink)
    shifted = jax.random.randint(jax.random.fold_in(rng, 1), (twos,), 0, 1 << 20) % (room + 1)
    tallies = tallies.at[1:1 + 2 * twos:2].set(donor - shifted).at[2:2 + 2 * twos:2].set(sink + shifted)
    return tallies[jax.random.permutation(jax.random.fold_in(rng, 2), count)]


def routed_block(rng, own, number, rows, amount, top, bound, slope):
    order = jax.random.permutation(rng, amount)
    heavy_load, ordinary = portions_of(amount, rows * top, bound, slope, True), portions_of(amount, rows * top, bound, slope, False)
    places = jnp.arange(amount)

    def named(tallies, rotation):
        used = int((tallies > 0).sum())
        fixed = max(1, used // 4)
        moved = fixed + (places - fixed + rotation * (used - fixed)) % max(1, amount - fixed)
        return jnp.zeros((amount,), jnp.int32).at[order[jnp.where(places < fixed, places, moved)]].set(jnp.asarray(tallies, jnp.int32))

    tallies = jnp.where(number % 4 == 0, named(heavy_load, number // 4), named(ordinary, number - number // 4 - 1))
    mixed = jax.random.permutation(jax.random.fold_in(own, 3), amount)
    donor, taker = mixed[0:amount // 2 * 2:2], mixed[1:amount // 2 * 2:2]
    room = jnp.minimum(tallies[donor] - 1, bound - tallies[taker]) // 2
    room = jnp.where((donor == order[0]) | (taker == order[0]) | (tallies[taker] == 0), 0, jnp.maximum(room, 0))
    moved = jax.random.randint(jax.random.fold_in(own, 4), (amount // 2,), 0, 1 << 20) % (room + 1)
    tallies = tallies.at[donor].add(-moved).at[taker].add(moved)
    members = jnp.searchsorted(jnp.cumsum(tallies), jnp.arange(rows * top), side="right").astype(jnp.int32)
    table = members.reshape(top, rows).T
    table = table[jax.random.permutation(jax.random.fold_in(own, 1), rows)]
    rotation = jax.random.randint(jax.random.fold_in(own, 2), (rows, 1), 0, top)
    return jnp.take_along_axis(table, (jnp.arange(top)[None, :] + rotation) % top, axis=1)


def portions_of(amount, total, most, slope, full):
    loads = [(1 << 20) // math.isqrt(rank ** slope) + 1 for rank in range(1, amount + 1)]
    largest = most if full else min(most, max(-(-total // amount), total * loads[0] // sum(loads)))
    least = 1 if total - largest >= amount - 1 else 0
    given, surplus = [largest] + [least] * (amount - 1), total - largest - least * (amount - 1)
    while surplus > 0:
        movable = [i for i in range(1, amount) if given[i] < largest] or [i for i in range(1, amount) if given[i] < most]
        pool, budget = sum([loads[i] for i in movable]), surplus
        for i in movable:
            addition = min(most - given[i], max(1, budget * loads[i] // pool), surplus)
            given[i] = given[i] + addition
            surplus = surplus - addition
    return np.array(given)


def bell_draw(key, extent, spread, reach, pieces=(), kind=jnp.bfloat16):
    drawn = jax.random.normal(key, extent, jnp.float32) * spread
    if len(pieces) > 0:
        drawn = levels(key, extent, pieces, -0.22, 0.18) * drawn
    return jnp.clip(drawn, min=-reach, max=reach).astype(kind)


def setup_inputs(seed: int = 0) -> dict:
    streams_of = jax.random.split(jax.random.key(seed), 12)
    patches = bell_draw(streams_of[0], (N_EXP, SHARDS, MERGE * IMG_CAP, VIT), 1.0, 6.0, ((0, 8), (1, 4)))
    image_counts = jax.vmap(lambda own: ragged(own, SHARDS, SEQ_TOK, IMG_CAP, 2))(jax.random.split(streams_of[1], N_EXP)).reshape((N_EXP, SHARDS)).astype(jnp.int32)
    image_order = jax.vmap(lambda own: jax.random.permutation(own, SHARDS))(jax.random.split(streams_of[2], N_EXP)).reshape((N_EXP, SHARDS)).astype(jnp.int32)
    w_merge = bell_draw(streams_of[3], (MERGE * VIT, PROJ_H), (MERGE * VIT) ** -0.5, 0.09375, ((1, 4),))
    w_proj_out = bell_draw(streams_of[4], (N_SEQ, N_ENC, PROJ_H // (N_SEQ * N_ENC), D), PROJ_H ** -0.5, 0.109375, ((1, 2), (3, 2)))
    routes_keys = jax.random.split(jax.random.fold_in(streams_of[5], 1), TOKENS // TOK_DEV)
    routes_turns = jax.random.permutation(jax.random.fold_in(streams_of[5], 3), TOKENS // TOK_DEV)
    routes = jax.vmap(lambda own, number: routed_block(jax.random.fold_in(streams_of[5], 2), own, number, TOK_DEV, ALL_EXPERTS, TOP, CAP, 0))(routes_keys, routes_turns).reshape((TOKENS, TOP))
    route_weight = jnp.clip(0.2 + 0.8 * jax.random.uniform(streams_of[6], (TOKENS, TOP), jnp.float32) ** levels(streams_of[6], (TOKENS, TOP), ((0, 16),), -0.2, 0.2), 0.2, 1.0)
    expert_place = draw_expert_place(jax.random.fold_in(streams_of[11], 71), 0)
    w_gate = bell_draw(streams_of[8], (EXPERTS, D, EXP_H), D ** -0.5, 0.0625, ((0, 8), (2, 2)))
    w_up = bell_draw(streams_of[9], (EXPERTS, D, EXP_H), D ** -0.5, 0.0625, ((0, 8), (2, 2)))
    w_down = bell_draw(streams_of[10], (EXPERTS, EXP_H, D), EXP_H ** -0.5, 0.1875, ((0, 8), (1, 2)))
    return dict(patches=patches, image_counts=image_counts, image_order=image_order, w_merge=w_merge, w_proj_out=w_proj_out, routes=routes, route_weight=route_weight, expert_place=expert_place, w_gate=w_gate, w_up=w_up, w_down=w_down)


def layer_norm(values):
    centre_mean = lax.optimization_barrier(jnp.mean(values, axis=-1, keepdims=True))
    centred = values - centre_mean
    variance = lax.optimization_barrier(jnp.mean(centred * centred, axis=-1, keepdims=True))
    return centred * lax.rsqrt(variance + 1e-06)

def sequence_rows(counts, order, seq_len, image_cap):
    shard_total = counts.shape[0]
    shard_ids = jnp.arange(shard_total, dtype=jnp.int32)
    picked = (order[:, None] == shard_ids[None, :]).astype(jnp.int32)
    ordered = lax.optimization_barrier(jnp.sum(picked * counts[None, :], axis=1))
    run_ends = jnp.cumsum(ordered)
    run_starts = run_ends - ordered
    position = jnp.arange(seq_len, dtype=jnp.int32)
    image_slot = lax.optimization_barrier(jnp.sum((position[:, None] >= run_ends[None, :]).astype(jnp.int32), axis=1))
    selected = (image_slot[:, None] == shard_ids[None, :]).astype(jnp.int32)
    shard_id = lax.optimization_barrier(jnp.sum(selected * order[None, :], axis=1))
    first_row = lax.optimization_barrier(jnp.sum(selected * run_starts[None, :], axis=1))
    return (shard_id * image_cap + position - first_row).astype(jnp.int32)

def slot_table(routes, weights, place, n_dest, cap):
    token_count, top_count = routes.shape
    target = jnp.take(place, routes.reshape(-1), axis=0)
    onehot = (target[:, None] == jnp.arange(n_dest, dtype=jnp.int32)[None, :]).astype(jnp.int32)
    rank_here = lax.optimization_barrier(jnp.sum((jnp.cumsum(onehot, axis=0) - 1) * onehot, axis=1))
    slot_id = jnp.where(target >= 0, target * cap + rank_here, -1)
    matches = slot_id[None, :] == jnp.arange(n_dest * cap, dtype=jnp.int32)[:, None]
    token_of = jnp.arange(token_count * top_count, dtype=jnp.int32) // top_count
    slot_tok = lax.optimization_barrier(jnp.sum(jnp.where(matches, token_of[None, :], 0), axis=1)).astype(jnp.int32)
    live_slot = jnp.any(matches, axis=1)
    mixing = jnp.where(matches, weights.reshape(-1)[None, :], jnp.zeros((), weights.dtype))
    mixing = lax.optimization_barrier(jnp.sum(mixing.reshape(n_dest * cap, token_count, top_count), axis=2))
    return (slot_tok, live_slot, mixing)

def kept_bf16(values):
    return lax.optimization_barrier(values.astype(jnp.bfloat16)).astype(jnp.float32)

def reference(patches, image_counts, image_order, w_merge, w_proj_out, routes, route_weight, expert_place, w_gate, w_up, w_down):
    proj_block = PROJ_H // (N_SEQ * N_ENC)
    hidden_block = EXP_H // N_SEQ
    weight_out = w_proj_out.astype(jnp.float32)

    def project(operands):
        patch, counts, order = operands
        normed = layer_norm(patch.astype(jnp.float32)).astype(jnp.bfloat16)
        merged = normed.reshape(SHARDS * IMG_CAP, MERGE * VIT)
        inner_act = jax.nn.gelu(jnp.dot(merged, w_merge, preferred_element_type=jnp.float32), approximate=False).astype(jnp.bfloat16)
        placed = jnp.take(inner_act, sequence_rows(counts, order, SEQ_TOK, IMG_CAP), axis=0)
        blocks_in = placed.reshape(SEQ_TOK, N_SEQ, N_ENC, proj_block).astype(jnp.float32)
        partial_out = jnp.einsum('tsck,sckd->ctd', blocks_in, weight_out, precision=lax.Precision.HIGHEST)
        partial_out = kept_bf16(partial_out)
        return lax.optimization_barrier(jnp.sum(partial_out, axis=0)).astype(jnp.bfloat16)
    x_all = lax.map(project, (patches, image_counts, image_order)).reshape(TOKENS, D)
    block_count = N_EXP * N_ENC
    slot_tok, live_slot, mixing = jax.vmap(partial(slot_table, place=expert_place, n_dest=EXPERTS, cap=CAP))(routes.reshape(block_count, TOK_DEV, TOP), route_weight.reshape(block_count, TOK_DEV, TOP))
    x_blocks = x_all.reshape(block_count, TOK_DEV, D)
    slot_rows = jax.vmap(partial(jnp.take, axis=0))(x_blocks, slot_tok)
    slot_rows = jnp.where(live_slot[:, :, None], slot_rows, jnp.zeros((), jnp.bfloat16))
    slot_rows = slot_rows.reshape(block_count, EXPERTS, CAP, D).transpose(1, 0, 2, 3).reshape(EXPERTS, block_count * CAP, D)

    def expert(operands):
        inputs, gate_w, up_w, down_w = operands
        squares = lax.optimization_barrier(jnp.sum(jnp.square(inputs.astype(jnp.float32)), axis=1, keepdims=True))
        inv_rms = lax.rsqrt(squares / D + 1e-06)
        gate_sum = jnp.dot(inputs, gate_w, preferred_element_type=jnp.float32) * inv_rms
        up_sum = jnp.dot(inputs, up_w, preferred_element_type=jnp.float32) * inv_rms
        hidden = (jax.nn.silu(gate_sum) * up_sum).astype(jnp.bfloat16)
        total = jnp.zeros((inputs.shape[0], D), jnp.float32)
        for block in range(N_SEQ):
            lower = block * hidden_block
            term = jnp.dot(hidden[:, lower:lower + hidden_block], down_w[lower:lower + hidden_block], preferred_element_type=jnp.float32)
            total = total + kept_bf16(term)
        return total.astype(jnp.bfloat16)
    outputs = lax.map(expert, (slot_rows, w_gate, w_up, w_down))
    outputs = outputs.reshape(EXPERTS, block_count, CAP, D).transpose(1, 0, 2, 3).reshape(block_count, EXPERTS * CAP, D)
    combined = jnp.einsum('bst,bsd->btd', mixing, outputs.astype(jnp.float32), precision=lax.Precision.HIGHEST)
    hidden_out = (x_blocks.astype(jnp.float32) + combined).astype(jnp.bfloat16).reshape(TOKENS, D)
    filled = live_slot.astype(jnp.float32).reshape(N_EXP, N_ENC, EXPERTS, CAP)
    expert_load = lax.optimization_barrier(jnp.sum(filled, axis=(0, 3))).T * (ALL_EXPERTS / (N_EXP * TOK_DEV * TOP))
    return (hidden_out, expert_load)
```

```python
import functools

import jax
import jax.numpy as jnp
from jax import lax
from jax.experimental import pallas as pl
from jax.experimental.pallas import tpu as pltpu
from jax.sharding import PartitionSpec as P

MERGE = 4
CAP = 3
PIECE = 4
GROUP = 8
BF = jnp.bfloat16
F32 = jnp.float32
I32 = jnp.int32
MESH = pl.DeviceIdType.MESH


def up(value, step):
    return -(-value // step) * step


def iota(shape, axis):
    return lax.broadcasted_iota(I32, shape, axis)


def mm(a, b):
    return jnp.dot(a, b, preferred_element_type=F32)


def kernel(
    dims,
    counts_ref, order_ref, patches_ref, wm_hbm, w2_hbm, routes_ref, weight_ref, place_ref,
    wg_hbm, wu_hbm, wd_hbm,
    out_ref, load_ref,
    raw, nb, wm, w2, wg, wu, wd, acc1, ib, place_mat, acc2, psend, precv, xbuf,
    slot_send, rs, lf, dsend, drecv, ysend, yrecv, mix, gsel, gcnt,
    raw_sem, wm_sem, w2_sem, wx_sem,
    ny_s, ny_r, nc_s, nc_r, ib_s, ib_r, ps_s, ps_r, sl_s, sl_r, fw_s, fw_r, dn_s, dn_r, bk_s, bk_r,
    own_sem,
):
    ns, ne, nc_enc, cap_img, rp, wr, vit, units, cols, chunk, tok, top, n_all, hid = dims
    nchunk = cols // chunk
    s, e, c = lax.axis_index("seq"), lax.axis_index("exp"), lax.axis_index("enc")
    other = lax.rem(c + 1, nc_enc)

    def to_seq(j):
        return {"seq": lax.rem(s + j, ns)}

    def from_seq(j):
        return lax.rem(s + ns - j, ns)

    core = {"enc": other}

    def to_exp(k):
        return {"exp": lax.rem(e + k, ne)}

    def remote(src, dst, send, recv, dev):
        return pltpu.make_async_remote_copy(
            src_ref=src, dst_ref=dst, send_sem=send, recv_sem=recv, device_id=dev,
            device_id_type=MESH,
        )

    raw_copy = pltpu.make_async_copy(patches_ref.at[0, 0], raw, raw_sem)
    raw_copy.start()
    wm_copies = [
        pltpu.make_async_copy(
            wm_hbm.at[pl.ds(m * vit, vit)], wm.at[pl.ds(m * vit, vit)], wm_sem.at[m]
        )
        for m in range(MERGE)
    ]
    for cp in wm_copies:
        cp.start()
    w2_copies = []
    for j in range(ns):
        b = from_seq(j)
        w2_copies.append(pltpu.make_async_copy(w2_hbm.at[b, 0], w2.at[b], w2_sem.at[j]))
    for cp in w2_copies:
        cp.start()
    wx_copies = [
        pltpu.make_async_copy(wg_hbm.at[0], wg, wx_sem.at[0]),
        pltpu.make_async_copy(wu_hbm.at[0], wu, wx_sem.at[1]),
        pltpu.make_async_copy(wd_hbm.at[0], wd, wx_sem.at[2]),
    ]
    for cp in wx_copies:
        cp.start()

    barrier = pltpu.get_barrier_semaphore()
    for j in range(1, ns):
        pl.semaphore_signal(barrier, inc=1, device_id=to_seq(j), device_id_type=MESH)
    pl.semaphore_signal(barrier, inc=1, device_id=core, device_id_type=MESH)
    for k in range(1, ne):
        pl.semaphore_signal(barrier, inc=1, device_id=to_exp(k), device_id_type=MESH)

    raw_copy.wait()
    values = raw[...].astype(F32)
    centred = values - jnp.mean(values, axis=1, keepdims=True)
    variance = jnp.mean(centred * centred, axis=1, keepdims=True)
    normed = (centred * lax.rsqrt(variance + 1e-06)).astype(BF)
    rows_in = cap_img * MERGE
    k_i, r_i = iota((rp, rows_in), 0), iota((rp, rows_in), 1)
    for m in range(MERGE):
        pick = jnp.where((k_i < cap_img) & (r_i == k_i * MERGE + m), 1.0, 0.0).astype(BF)
        nb[s, c, m] = mm(pick, normed).astype(BF)

    pl.semaphore_wait(barrier, ns - 1 + 1 + ne - 1)

    def nb_at(p, cc, m):
        return nb.at[p, cc, m, pl.ds(0, wr)]

    pending = []
    for m in range(MERGE):
        for j in range(1, ns):
            cp = remote(nb_at(s, c, m), nb_at(s, c, m), ny_s.at[j, m], ny_r.at[j, m], to_seq(j))
            cp.start()
            pending.append(cp)
        cp = remote(nb_at(s, c, m), nb_at(s, c, m), nc_s.at[0, m], nc_r.at[0, m], core)
        cp.start()
        pending.append(cp)

    live = lax.rem(iota((nc_enc * rp, 1), 0), rp) < cap_img

    def finish_inner(p):
        a = acc1[...]
        inner = 0.5 * a * (1.0 + lax.erf(a * 0.7071067811865476))
        ib[s, p] = jnp.where(live, inner, 0.0).astype(BF)

    def send_inner(p, j0):
        for j in range(1, ns):
            cp = remote(ib.at[s, p], ib.at[s, p], ib_s.at[j, j0], ib_r.at[j, j0], to_seq(j))
            cp.start()
            pending.append(cp)

    def mm1(p, m):
        lhs = nb[p, :, m].reshape(nc_enc * rp, vit)
        term = mm(lhs, wm[pl.ds(m * vit, vit), :])
        if m == 0:
            acc1[...] = term
        else:
            acc1[...] += term

    ncol = mix.shape[1] // 3
    place = place_ref[...]
    d_of = iota((ncol, n_all), 0) // GROUP
    held = jnp.where(place == d_of, 1.0, 0.0).astype(BF)
    number = iota((GROUP, n_all), 1)
    contract_last = (((1,), (1,)), ((), ()))
    high = lax.dot_general(
        (number // 16).astype(F32).astype(BF), held, contract_last, preferred_element_type=F32
    )
    low = lax.dot_general(
        lax.rem(number, 16).astype(F32).astype(BF), held, contract_last,
        preferred_element_type=F32,
    )
    expert = (high * 16.0 + low)[0:1].astype(I32)
    col = iota((1, ncol), 1)
    expert = jnp.where(col < ne * GROUP, expert, -1)
    q_of = lax.rem(col, GROUP)
    named = jnp.zeros((tok, ncol), F32)
    amount = jnp.zeros((tok, ncol), F32)
    for k in range(top):
        match = routes_ref[:, k : k + 1] == expert
        named = jnp.where(match, 1.0, named)
        amount = amount + jnp.where(match, weight_ref[:, k : k + 1], 0.0)
    earlier = jnp.where(iota((tok, tok), 1) < iota((tok, tok), 0), 1.0, 0.0).astype(BF)
    rank = mm(earlier, named.astype(BF))
    chosen = jnp.where((rank == q_of.astype(F32)) & (q_of < CAP), named, 0.0)
    mixing = chosen * amount
    part_a = mixing.astype(BF)
    rest = mixing - part_a.astype(F32)
    part_b = rest.astype(BF)
    part_c = (rest - part_b.astype(F32)).astype(BF)
    mix[:, 0:ncol] = part_a
    mix[:, ncol : 2 * ncol] = part_b
    mix[:, 2 * ncol : 3 * ncol] = part_c
    gsel[...] = jnp.transpose(chosen).astype(BF)
    counted = jnp.transpose(jnp.where(q_of == CAP, named, 0.0))
    gcnt[...] = jnp.broadcast_to(jnp.sum(counted, axis=1, keepdims=True), gcnt.shape)
    lf[...] = jnp.zeros(lf.shape, F32)

    shard_total = ns * nc_enc
    starts, run = [], jnp.int32(0)
    for i in range(shard_total):
        starts.append(run)
        o_i = order_ref[0, i]
        for j in range(shard_total):
            run = run + jnp.where(o_i == j, counts_ref[0, j], 0)
    seq_len = tok * nc_enc
    position = lax.rem(iota((seq_len, rp), 0) + other * tok, seq_len)
    k_row = iota((seq_len, rp), 1)
    for j in range(shard_total):
        first = jnp.int32(0)
        for i in range(shard_total):
            first = first + jnp.where(order_ref[0, i] == j, starts[i], 0)
        hit = (position - first == k_row) & (k_row < counts_ref[0, j])
        place_mat[j] = jnp.where(hit, 1.0, 0.0).astype(BF)

    for m in range(MERGE):
        wm_copies[m].wait()
        remote(
            nb_at(s, other, m), nb_at(s, other, m), nc_s.at[0, m], nc_r.at[0, m], core
        ).wait_recv()
        mm1(s, m)
    finish_inner(s)
    send_inner(s, 0)
    for j in range(1, ns):
        p = from_seq(j)
        for m in range(MERGE):
            remote(
                nb_at(p, c, m), nb_at(p, c, m), ny_s.at[j, m], ny_r.at[j, m], to_seq(j)
            ).wait_recv()
            cp = remote(nb_at(p, c, m), nb_at(p, c, m), nc_s.at[j, m], nc_r.at[j, m], core)
            cp.start()
            pending.append(cp)
            remote(
                nb_at(p, other, m), nb_at(p, other, m), nc_s.at[j, m], nc_r.at[j, m], core
            ).wait_recv()
            mm1(p, m)
        finish_inner(p)
        send_inner(p, j)

    def placed_of(b):
        total = jnp.zeros((seq_len, units), F32)
        for p in range(ns):
            for cc in range(nc_enc):
                total += mm(place_mat[p * nc_enc + cc], ib[b, p, pl.ds(cc * rp, rp)])
        return total.astype(BF)

    def columns_at(n):
        return pl.ds(pl.multiple_of(n * chunk, chunk), chunk)

    for j in range(ns):
        b = from_seq(j)
        if j > 0:
            for t in range(ns):
                src_p = lax.rem(b + ns - t, ns)
                remote(
                    ib.at[b, src_p], ib.at[b, src_p], ib_s.at[j, t], ib_r.at[j, t], to_seq(j)
                ).wait_recv()
        w2_copies[j].wait()
        placed = placed_of(b)
        for n in range(nchunk):
            term = mm(placed, w2[b, :, n * chunk : (n + 1) * chunk])
            if j > 0:
                term = acc2[n] + term
            if j < ns - 1:
                acc2[n] = term
            else:
                psend[n] = term[0:tok].astype(BF)
                xbuf[n] = term[tok : 2 * tok].astype(BF)
                cp = remote(psend.at[n], precv.at[n], ps_s.at[n], ps_r.at[n], core)
                cp.start()
                pending.append(cp)

    flag_row = lax.rem(iota((ncol, 1), 0), GROUP) == CAP
    for n in range(nchunk):
        remote(psend.at[n], precv.at[n], ps_s.at[n], ps_r.at[n], core).wait_recv()
        x = (xbuf[n].astype(F32) + precv[n].astype(F32)).astype(BF)
        xbuf[n] = x
        rows = jnp.where(flag_row, gcnt[:, 0:1], mm(gsel[...], x))
        for d in range(ne):
            slot_send[d, :, n * chunk : (n + 1) * chunk] = rows[
                d * GROUP : d * GROUP + PIECE
            ].astype(BF)

    for k in range(1, ne):
        dst = lax.rem(e + k, ne)
        cp = remote(slot_send.at[dst], rs.at[s, e], sl_s.at[k], sl_r.at[k], to_exp(k))
        cp.start()
        pending.append(cp)
    own_copy = pltpu.make_async_copy(slot_send.at[e], rs.at[s, e], own_sem.at[0])
    own_copy.start()
    for k in range(ne):
        src = lax.rem(e + ne - k, ne)
        if k == 0:
            own_copy.wait()
        else:
            remote(slot_send.at[e], rs.at[s, src], sl_s.at[k], sl_r.at[k], to_exp(k)).wait_recv()
        for j in range(1, ns):
            cp = remote(rs.at[s, src], rs.at[s, src], fw_s.at[j, k], fw_r.at[j, k], to_seq(j))
            cp.start()
            pending.append(cp)

    rows_e = ne * GROUP
    gate_sum = jnp.zeros((rows_e, hid), F32)
    up_sum = jnp.zeros((rows_e, hid), F32)
    squares = jnp.zeros((rows_e, 1), F32)
    wx_copies[0].wait()
    wx_copies[1].wait()
    for j in range(ns):
        p = from_seq(j)
        if j > 0:
            for k in range(ne):
                src = lax.rem(e + ne - k, ne)
                remote(
                    rs.at[p, src], rs.at[p, src], fw_s.at[j, k], fw_r.at[j, k], to_seq(j)
                ).wait_recv()
        for d in range(ne):
            lf[d * GROUP : d * GROUP + PIECE] = rs[p, d].astype(F32)
        if j == 0:
            tile = lf[:, 0:128]
            flagged = (lax.rem(iota(tile.shape, 0), GROUP) == CAP) & (iota(tile.shape, 1) == 0)
            filled = jnp.where(flagged, tile, 0.0)
            filled = jnp.sum(jnp.sum(filled, axis=1, keepdims=True), axis=0, keepdims=True)
            load_ref[...] = filled * (n_all / (ne * tok * top))
        for n in range(nchunk):
            block = lf[:, n * chunk : (n + 1) * chunk]
            squares = squares + jnp.sum(block * block, axis=1, keepdims=True)
            lhs = block.astype(BF)
            at = pl.ds(pl.multiple_of(p * cols + n * chunk, chunk), chunk)
            gate_sum = gate_sum + mm(lhs, wg[at, :])
            up_sum = up_sum + mm(lhs, wu[at, :])
    inv_rms = lax.rsqrt(squares / (ns * cols) + 1e-06)
    gate = gate_sum * inv_rms
    hidden = (gate / (1.0 + jnp.exp(-gate)) * (up_sum * inv_rms)).astype(BF)
    wx_copies[2].wait()

    for j in list(range(1, ns)) + [0]:
        p = lax.rem(s + j, ns)
        for n in range(nchunk):
            at = pl.ds(pl.multiple_of(p * cols + n * chunk, chunk), chunk)
            term = mm(hidden, wd[:, at])
            for d in range(ne):
                dsend[j, d, :, n * chunk : (n + 1) * chunk] = term[
                    d * GROUP : d * GROUP + PIECE
                ].astype(BF)
        if j > 0:
            cp = remote(dsend.at[j], drecv.at[j], dn_s.at[j], dn_r.at[j], to_seq(j))
            cp.start()
            pending.append(cp)
    for j in range(1, ns):
        remote(dsend.at[j], drecv.at[j], dn_s.at[j], dn_r.at[j], to_seq(j)).wait_recv()
    total = dsend[0].astype(F32)
    for j in range(1, ns):
        total = total + drecv[j].astype(F32)
    ysend[...] = total.astype(BF)
    for k in range(1, ne):
        dst = lax.rem(e + k, ne)
        cp = remote(ysend.at[dst], yrecv.at[e], bk_s.at[k], bk_r.at[k], to_exp(k))
        cp.start()
        pending.append(cp)
    back_copy = pltpu.make_async_copy(ysend.at[e], yrecv.at[e], own_sem.at[1])
    back_copy.start()
    back_copy.wait()
    for k in range(1, ne):
        src = lax.rem(e + ne - k, ne)
        remote(ysend.at[e], yrecv.at[src], bk_s.at[k], bk_r.at[k], to_exp(k)).wait_recv()
    for d in range(ne):
        lf[d * GROUP : d * GROUP + PIECE] = yrecv[d].astype(F32)
    for n in range(nchunk):
        y = lf[:, n * chunk : (n + 1) * chunk].astype(BF)
        if ncol > rows_e:
            y = jnp.concatenate([y, jnp.zeros((ncol - rows_e, chunk), BF)], axis=0)
        combined = mm(mix[...], jnp.concatenate([y, y, y], axis=0))
        out_ref[:, n * chunk : (n + 1) * chunk] = (xbuf[n].astype(F32) + combined).astype(BF)
    for cp in pending:
        cp.wait_send()


def shards(mesh_shape, *args):
    (patches, image_counts, image_order, w_merge, w_proj_out, routes, route_weight,
     expert_place, w_gate, w_up, w_down) = args
    ns, ne, nc = mesh_shape["seq"], mesh_shape["exp"], mesh_shape["enc"]
    rows_in, vit = patches.shape[2:]
    cap_img = rows_in // MERGE
    rp = up(cap_img, 16)
    wr = up(cap_img, 8)
    units = w_merge.shape[1]
    cols = w_proj_out.shape[3]
    tok, top = routes.shape
    n_all = expert_place.shape[0]
    hid = w_gate.shape[2]
    chunk = [w for w in (512, 256, 128) if cols % w == 0][0]
    nchunk = cols // chunk
    ncol = up(ne * GROUP, 128)
    dims = (ns, ne, nc, cap_img, rp, wr, vit, units, cols, chunk, tok, top, n_all, hid)
    anyspec = pl.BlockSpec(memory_space=pl.ANY)
    vmem = pl.BlockSpec(memory_space=pltpu.VMEM)
    smem = pl.BlockSpec(memory_space=pltpu.SMEM)
    dma = pltpu.SemaphoreType.DMA
    V = pltpu.VMEM
    scratch = [
        V((rows_in, vit), BF),
        V((ns, nc, MERGE, rp, vit), BF),
        V((MERGE * vit, units), BF),
        V((ns, units, cols), BF),
        V((ns * cols, hid), BF),
        V((ns * cols, hid), BF),
        V((hid, ns * cols), BF),
        V((nc * rp, units), F32),
        V((ns, ns, nc * rp, units), BF),
        V((ns * nc, tok * nc, rp), BF),
        V((nchunk, tok * nc, chunk), F32),
        V((nchunk, tok, chunk), BF),
        V((nchunk, tok, chunk), BF),
        V((nchunk, tok, chunk), BF),
        V((ne, PIECE, cols), BF),
        V((ns, ne, PIECE, cols), BF),
        V((ne * GROUP, cols), F32),
        V((ns, ne, PIECE, cols), BF),
        V((ns, ne, PIECE, cols), BF),
        V((ne, PIECE, cols), BF),
        V((ne, PIECE, cols), BF),
        V((tok, 3 * ncol), BF),
        V((ncol, tok), BF),
        V((ncol, 128), F32),
        dma, dma((MERGE,)), dma((ns,)), dma((3,)),
        dma((ns, MERGE)), dma((ns, MERGE)), dma((ns, MERGE)), dma((ns, MERGE)),
        dma((ns, ns)), dma((ns, ns)), dma((nchunk,)), dma((nchunk,)),
        dma((ne,)), dma((ne,)), dma((ns, ne)), dma((ns, ne)),
        dma((ns,)), dma((ns,)), dma((ne,)), dma((ne,)),
        dma((2,)),
    ]
    return pl.pallas_call(
        functools.partial(kernel, dims),
        out_shape=(
            jax.ShapeDtypeStruct((tok, cols), BF),
            jax.ShapeDtypeStruct((1, 1), F32),
        ),
        in_specs=[smem, smem, anyspec, anyspec, anyspec, vmem, vmem, vmem] + [anyspec] * 3,
        out_specs=(vmem, vmem),
        scratch_shapes=scratch,
        compiler_params=pltpu.CompilerParams(
            collective_id=0, has_side_effects=True, vmem_limit_bytes=67043328
        ),
        name="step",
    )(
        image_counts, image_order, patches, w_merge, w_proj_out, routes, route_weight,
        expert_place.reshape(1, n_all), w_gate, w_up, w_down,
    )


def solution(mesh):
    in_specs = (
        P("exp", ("seq", "enc"), None, None),
        P("exp", None),
        P("exp", None),
        P(None, ("seq", "enc")),
        P(None, "enc", None, "seq"),
        P(("exp", "enc"), None),
        P(("exp", "enc"), None),
        P(),
        P("exp", None, "seq"),
        P("exp", None, "seq"),
        P("exp", "seq", None),
    )
    out_specs = (P(("exp", "enc"), "seq"), P("exp", "enc"))
    body = functools.partial(shards, dict(mesh.shape))
    return jax.shard_map(body, mesh=mesh, in_specs=in_specs, out_specs=out_specs, check_vma=False)
```

```python
import functools

import jax
import jax.numpy as jnp
from jax import lax
from jax.experimental import pallas as pl
from jax.experimental.pallas import tpu as pltpu
from jax.sharding import PartitionSpec as P

MERGE = 4
CAP = 3
PIECE = 4
GROUP = 8
BF = jnp.bfloat16
F32 = jnp.float32
I32 = jnp.int32
MESH = pl.DeviceIdType.MESH


def up(value, step):
    return -(-value // step) * step


def iota(shape, axis):
    return lax.broadcasted_iota(I32, shape, axis)


def mm(a, b):
    return jnp.dot(a, b, preferred_element_type=F32)


def kernel(
    dims,
    counts_ref, order_ref, patches_ref, wm_hbm, w2_hbm, routes_ref, weight_ref, place_ref,
    wg_hbm, wu_hbm, wd_hbm,
    out_ref, load_ref,
    raw, nb, wm, w2, wg, wu, wd, acc1, ib, place_mat, acc2, psend, precv, xbuf,
    slot_send, rs, lf, dsend, drecv, ysend, yrecv, mix, gsel, gcnt,
    raw_sem, wm_sem, w2_sem, wx_sem,
    ny_s, ny_r, nc_s, nc_r, ib_s, ib_r, ps_s, ps_r, sl_s, sl_r, fw_s, fw_r, dn_s, dn_r, bk_s, bk_r,
    own_sem,
):
    ns, ne, nc_enc, cap_img, rp, wr, vit, units, cols, chunk, tok, top, n_all, hid = dims
    nchunk = cols // chunk
    s, e, c = lax.axis_index("seq"), lax.axis_index("exp"), lax.axis_index("enc")
    other = lax.rem(c + 1, nc_enc)

    def to_seq(j):
        return {"seq": lax.rem(s + j, ns)}

    def from_seq(j):
        return lax.rem(s + ns - j, ns)

    core = {"enc": other}

    def to_exp(k):
        return {"exp": lax.rem(e + k, ne)}

    def remote(src, dst, send, recv, dev):
        return pltpu.make_async_remote_copy(
            src_ref=src, dst_ref=dst, send_sem=send, recv_sem=recv, device_id=dev,
            device_id_type=MESH,
        )

    raw_copy = pltpu.make_async_copy(patches_ref.at[0, 0], raw, raw_sem)
    raw_copy.start()
    wm_copies = [
        pltpu.make_async_copy(
            wm_hbm.at[:, pl.ds(m * vit, vit)], wm.at[m], wm_sem.at[m]
        )
        for m in range(MERGE)
    ]
    for cp in wm_copies:
        cp.start()
    w2_copies = []
    for j in range(ns):
        b = from_seq(j)
        w2_copies.append(pltpu.make_async_copy(w2_hbm.at[b, 0], w2.at[b], w2_sem.at[j]))
    for cp in w2_copies:
        cp.start()
    wx_copies = [
        pltpu.make_async_copy(wg_hbm.at[0], wg, wx_sem.at[0]),
        pltpu.make_async_copy(wu_hbm.at[0], wu, wx_sem.at[1]),
        pltpu.make_async_copy(wd_hbm.at[0], wd, wx_sem.at[2]),
    ]
    for cp in wx_copies:
        cp.start()

    barrier = pltpu.get_barrier_semaphore()
    for j in range(1, ns):
        pl.semaphore_signal(barrier, inc=1, device_id=to_seq(j), device_id_type=MESH)
    pl.semaphore_signal(barrier, inc=1, device_id=core, device_id_type=MESH)
    for k in range(1, ne):
        pl.semaphore_signal(barrier, inc=1, device_id=to_exp(k), device_id_type=MESH)

    raw_copy.wait()
    values = raw[...].astype(F32)
    centred = values - jnp.mean(values, axis=1, keepdims=True)
    variance = jnp.mean(centred * centred, axis=1, keepdims=True)
    normed = (centred * lax.rsqrt(variance + 1e-06)).astype(BF)
    rows_in = cap_img * MERGE
    k_i, r_i = iota((rp, rows_in), 0), iota((rp, rows_in), 1)
    for m in range(MERGE):
        pick = jnp.where((k_i < cap_img) & (r_i == k_i * MERGE + m), 1.0, 0.0).astype(BF)
        nb[s, c, m] = mm(pick, normed).astype(BF)

    pl.semaphore_wait(barrier, ns - 1 + 1 + ne - 1)

    def nb_at(p, cc, m):
        return nb.at[p, cc, m, pl.ds(0, wr)]

    pending = []
    for m in range(MERGE):
        for j in range(1, ns):
            cp = remote(nb_at(s, c, m), nb_at(s, c, m), ny_s.at[j, m], ny_r.at[j, m], to_seq(j))
            cp.start()
            pending.append(cp)
        cp = remote(nb_at(s, c, m), nb_at(s, c, m), nc_s.at[0, m], nc_r.at[0, m], core)
        cp.start()
        pending.append(cp)

    live = lax.rem(iota((nc_enc * rp, 1), 0), rp) < cap_img

    def finish_inner(p):
        a = acc1[...]
        inner = 0.5 * a * (1.0 + lax.erf(a * 0.7071067811865476))
        ib[s, p] = jnp.where(live, inner, 0.0).astype(BF)

    def send_inner(p, j0):
        for j in range(1, ns):
            cp = remote(ib.at[s, p], ib.at[s, p], ib_s.at[j, j0], ib_r.at[j, j0], to_seq(j))
            cp.start()
            pending.append(cp)

    def mm1(p, m):
        lhs = nb[p, :, m].reshape(nc_enc * rp, vit)
        term = lax.dot_general(
            lhs, wm[m], (((1,), (1,)), ((), ())), preferred_element_type=F32
        )
        if m == 0:
            acc1[...] = term
        else:
            acc1[...] += term

    ncol = mix.shape[1] // 3
    place = place_ref[...].reshape(1, n_all)
    d_of = iota((ncol, n_all), 0) // GROUP
    number = iota((ncol, n_all), 1)
    expert = jnp.sum(jnp.where(place == d_of, number, 0), axis=1, keepdims=True)
    row = iota((ncol, 1), 0)
    expert = jnp.where(row < ne * GROUP, expert, -1)
    q_of = lax.rem(row, GROUP)
    named = jnp.zeros((ncol, tok), F32)
    amount = jnp.zeros((ncol, tok), F32)
    for k in range(top):
        match = routes_ref[k : k + 1, :] == expert
        named = jnp.where(match, 1.0, named)
        amount = amount + jnp.where(match, weight_ref[k : k + 1, :], 0.0)
    earlier = jnp.where(iota((tok, tok), 0) < iota((tok, tok), 1), 1.0, 0.0).astype(BF)
    rank = mm(named.astype(BF), earlier)
    chosen = jnp.where((rank == q_of.astype(F32)) & (q_of < CAP), named, 0.0)
    mixing = jnp.transpose(chosen * amount)
    part_a = mixing.astype(BF)
    rest = mixing - part_a.astype(F32)
    part_b = rest.astype(BF)
    part_c = (rest - part_b.astype(F32)).astype(BF)
    mix[:, 0:ncol] = part_a
    mix[:, ncol : 2 * ncol] = part_b
    mix[:, 2 * ncol : 3 * ncol] = part_c
    gsel[...] = chosen.astype(BF)
    counted = jnp.where(q_of == CAP, named, 0.0)
    gcnt[...] = jnp.broadcast_to(jnp.sum(counted, axis=1, keepdims=True), gcnt.shape)
    lf[...] = jnp.zeros(lf.shape, F32)

    shard_total = ns * nc_enc
    starts, run = [], jnp.int32(0)
    for i in range(shard_total):
        starts.append(run)
        o_i = order_ref[0, i]
        for j in range(shard_total):
            run = run + jnp.where(o_i == j, counts_ref[0, j], 0)
    seq_len = tok * nc_enc
    position = lax.rem(iota((seq_len, rp), 0) + other * tok, seq_len)
    k_row = iota((seq_len, rp), 1)
    for j in range(shard_total):
        first = jnp.int32(0)
        for i in range(shard_total):
            first = first + jnp.where(order_ref[0, i] == j, starts[i], 0)
        hit = (position - first == k_row) & (k_row < counts_ref[0, j])
        place_mat[j] = jnp.where(hit, 1.0, 0.0).astype(BF)

    for m in range(MERGE):
        wm_copies[m].wait()
        remote(
            nb_at(s, other, m), nb_at(s, other, m), nc_s.at[0, m], nc_r.at[0, m], core
        ).wait_recv()
        mm1(s, m)
    finish_inner(s)
    send_inner(s, 0)
    for j in range(1, ns):
        p = from_seq(j)
        for m in range(MERGE):
            remote(
                nb_at(p, c, m), nb_at(p, c, m), ny_s.at[j, m], ny_r.at[j, m], to_seq(j)
            ).wait_recv()
            cp = remote(nb_at(p, c, m), nb_at(p, c, m), nc_s.at[j, m], nc_r.at[j, m], core)
            cp.start()
            pending.append(cp)
            remote(
                nb_at(p, other, m), nb_at(p, other, m), nc_s.at[j, m], nc_r.at[j, m], core
            ).wait_recv()
            mm1(p, m)
        finish_inner(p)
        send_inner(p, j)

    def placed_of(b):
        total = jnp.zeros((seq_len, units), F32)
        for p in range(ns):
            for cc in range(nc_enc):
                total += mm(place_mat[p * nc_enc + cc], ib[b, p, pl.ds(cc * rp, rp)])
        return total.astype(BF)

    def columns_at(n):
        return pl.ds(pl.multiple_of(n * chunk, chunk), chunk)

    for j in range(ns):
        b = from_seq(j)
        if j > 0:
            for t in range(ns):
                src_p = lax.rem(b + ns - t, ns)
                remote(
                    ib.at[b, src_p], ib.at[b, src_p], ib_s.at[j, t], ib_r.at[j, t], to_seq(j)
                ).wait_recv()
        w2_copies[j].wait()
        placed = placed_of(b)
        for n in range(nchunk):
            term = mm(placed, w2[b, :, n * chunk : (n + 1) * chunk])
            if j > 0:
                term = acc2[n] + term
            if j < ns - 1:
                acc2[n] = term
            else:
                psend[n] = term[0:tok].astype(BF)
                xbuf[n] = term[tok : 2 * tok].astype(BF)
                cp = remote(psend.at[n], precv.at[n], ps_s.at[n], ps_r.at[n], core)
                cp.start()
                pending.append(cp)

    flag_row = lax.rem(iota((ncol, 1), 0), GROUP) == CAP
    for n in range(nchunk):
        remote(psend.at[n], precv.at[n], ps_s.at[n], ps_r.at[n], core).wait_recv()
        x = (xbuf[n].astype(F32) + precv[n].astype(F32)).astype(BF)
        xbuf[n] = x
        rows = jnp.where(flag_row, gcnt[:, 0:1], mm(gsel[...], x))
        for d in range(ne):
            slot_send[d, :, n * chunk : (n + 1) * chunk] = rows[
                d * GROUP : d * GROUP + PIECE
            ].astype(BF)

    for k in range(1, ne):
        dst = lax.rem(e + k, ne)
        cp = remote(slot_send.at[dst], rs.at[s, e], sl_s.at[k], sl_r.at[k], to_exp(k))
        cp.start()
        pending.append(cp)
    own_copy = pltpu.make_async_copy(slot_send.at[e], rs.at[s, e], own_sem.at[0])
    own_copy.start()
    for k in range(ne):
        src = lax.rem(e + ne - k, ne)
        if k == 0:
            own_copy.wait()
        else:
            remote(slot_send.at[e], rs.at[s, src], sl_s.at[k], sl_r.at[k], to_exp(k)).wait_recv()
        for j in range(1, ns):
            cp = remote(rs.at[s, src], rs.at[s, src], fw_s.at[j, k], fw_r.at[j, k], to_seq(j))
            cp.start()
            pending.append(cp)

    rows_e = ne * GROUP
    gate_sum = jnp.zeros((rows_e, hid), F32)
    up_sum = jnp.zeros((rows_e, hid), F32)
    squares = jnp.zeros((rows_e, 1), F32)
    wx_copies[0].wait()
    wx_copies[1].wait()
    for j in range(ns):
        p = from_seq(j)
        if j > 0:
            for k in range(ne):
                src = lax.rem(e + ne - k, ne)
                remote(
                    rs.at[p, src], rs.at[p, src], fw_s.at[j, k], fw_r.at[j, k], to_seq(j)
                ).wait_recv()
        for d in range(ne):
            lf[d * GROUP : d * GROUP + PIECE] = rs[p, d].astype(F32)
        if j == 0:
            tile = lf[:, 0:128]
            flagged = (lax.rem(iota(tile.shape, 0), GROUP) == CAP) & (iota(tile.shape, 1) == 0)
            filled = jnp.where(flagged, tile, 0.0)
            filled = jnp.sum(jnp.sum(filled, axis=1, keepdims=True), axis=0, keepdims=True)
            load_ref[...] = filled * (n_all / (ne * tok * top))
        for n in range(nchunk):
            block = lf[:, n * chunk : (n + 1) * chunk]
            squares = squares + jnp.sum(block * block, axis=1, keepdims=True)
            lhs = block.astype(BF)
            at = pl.ds(pl.multiple_of(p * cols + n * chunk, chunk), chunk)
            gate_sum = gate_sum + mm(lhs, wg[at, :])
            up_sum = up_sum + mm(lhs, wu[at, :])
    inv_rms = lax.rsqrt(squares / (ns * cols) + 1e-06)
    gate = gate_sum * inv_rms
    hidden = (gate / (1.0 + jnp.exp(-gate)) * (up_sum * inv_rms)).astype(BF)
    wx_copies[2].wait()

    for j in list(range(1, ns)) + [0]:
        p = lax.rem(s + j, ns)
        for n in range(nchunk):
            at = pl.ds(pl.multiple_of(p * cols + n * chunk, chunk), chunk)
            term = mm(hidden, wd[:, at])
            for d in range(ne):
                dsend[j, d, :, n * chunk : (n + 1) * chunk] = term[
                    d * GROUP : d * GROUP + PIECE
                ].astype(BF)
        if j > 0:
            cp = remote(dsend.at[j], drecv.at[j], dn_s.at[j], dn_r.at[j], to_seq(j))
            cp.start()
            pending.append(cp)
    for j in range(1, ns):
        remote(dsend.at[j], drecv.at[j], dn_s.at[j], dn_r.at[j], to_seq(j)).wait_recv()
    total = dsend[0].astype(F32)
    for j in range(1, ns):
        total = total + drecv[j].astype(F32)
    ysend[...] = total.astype(BF)
    for k in range(1, ne):
        dst = lax.rem(e + k, ne)
        cp = remote(ysend.at[dst], yrecv.at[e], bk_s.at[k], bk_r.at[k], to_exp(k))
        cp.start()
        pending.append(cp)
    back_copy = pltpu.make_async_copy(ysend.at[e], yrecv.at[e], own_sem.at[1])
    back_copy.start()
    back_copy.wait()
    for k in range(1, ne):
        src = lax.rem(e + ne - k, ne)
        remote(ysend.at[e], yrecv.at[src], bk_s.at[k], bk_r.at[k], to_exp(k)).wait_recv()
    for d in range(ne):
        lf[d * GROUP : d * GROUP + PIECE] = yrecv[d].astype(F32)
    for n in range(nchunk):
        y = lf[:, n * chunk : (n + 1) * chunk].astype(BF)
        if ncol > rows_e:
            y = jnp.concatenate([y, jnp.zeros((ncol - rows_e, chunk), BF)], axis=0)
        combined = mm(mix[...], jnp.concatenate([y, y, y], axis=0))
        out_ref[:, n * chunk : (n + 1) * chunk] = (xbuf[n].astype(F32) + combined).astype(BF)
    for cp in pending:
        cp.wait_send()


def shards(mesh_shape, *args):
    (patches, image_counts, image_order, w_merge, w_proj_out, routes, route_weight,
     expert_place, w_gate, w_up, w_down) = args
    ns, ne, nc = mesh_shape["seq"], mesh_shape["exp"], mesh_shape["enc"]
    rows_in, vit = patches.shape[2:]
    cap_img = rows_in // MERGE
    rp = up(cap_img, 16)
    wr = up(cap_img, 8)
    units = w_merge.shape[1]
    cols = w_proj_out.shape[3]
    tok, top = routes.shape
    n_all = expert_place.shape[0]
    hid = w_gate.shape[2]
    chunk = [w for w in (512, 256, 128) if cols % w == 0][0]
    nchunk = cols // chunk
    ncol = up(ne * GROUP, 128)
    dims = (ns, ne, nc, cap_img, rp, wr, vit, units, cols, chunk, tok, top, n_all, hid)
    anyspec = pl.BlockSpec(memory_space=pl.ANY)
    vmem = pl.BlockSpec(memory_space=pltpu.VMEM)
    smem = pl.BlockSpec(memory_space=pltpu.SMEM)
    dma = pltpu.SemaphoreType.DMA
    V = pltpu.VMEM
    scratch = [
        V((rows_in, vit), BF),
        V((ns, nc, MERGE, rp, vit), BF),
        V((MERGE, units, vit), BF),
        V((ns, units, cols), BF),
        V((ns * cols, hid), BF),
        V((ns * cols, hid), BF),
        V((hid, ns * cols), BF),
        V((nc * rp, units), F32),
        V((ns, ns, nc * rp, units), BF),
        V((ns * nc, tok * nc, rp), BF),
        V((nchunk, tok * nc, chunk), F32),
        V((nchunk, tok, chunk), BF),
        V((nchunk, tok, chunk), BF),
        V((nchunk, tok, chunk), BF),
        V((ne, PIECE, cols), BF),
        V((ns, ne, PIECE, cols), BF),
        V((ne * GROUP, cols), F32),
        V((ns, ne, PIECE, cols), BF),
        V((ns, ne, PIECE, cols), BF),
        V((ne, PIECE, cols), BF),
        V((ne, PIECE, cols), BF),
        V((tok, 3 * ncol), BF),
        V((ncol, tok), BF),
        V((ncol, 128), F32),
        dma, dma((MERGE,)), dma((ns,)), dma((3,)),
        dma((ns, MERGE)), dma((ns, MERGE)), dma((ns, MERGE)), dma((ns, MERGE)),
        dma((ns, ns)), dma((ns, ns)), dma((nchunk,)), dma((nchunk,)),
        dma((ne,)), dma((ne,)), dma((ns, ne)), dma((ns, ne)),
        dma((ns,)), dma((ns,)), dma((ne,)), dma((ne,)),
        dma((2,)),
    ]
    return pl.pallas_call(
        functools.partial(kernel, dims),
        out_shape=(
            jax.ShapeDtypeStruct((tok, cols), BF),
            jax.ShapeDtypeStruct((1, 1), F32),
        ),
        in_specs=[smem, smem, anyspec, anyspec, anyspec, vmem, vmem, vmem] + [anyspec] * 3,
        out_specs=(vmem, vmem),
        scratch_shapes=scratch,
        compiler_params=pltpu.CompilerParams(
            collective_id=0, has_side_effects=True, vmem_limit_bytes=67043328
        ),
        name="step",
    )(
        image_counts, image_order, patches, w_merge.T, w_proj_out, routes.T, route_weight.T,
        expert_place, w_gate, w_up, w_down,
    )


def solution(mesh):
    in_specs = (
        P("exp", ("seq", "enc"), None, None),
        P("exp", None),
        P("exp", None),
        P(None, ("seq", "enc")),
        P(None, "enc", None, "seq"),
        P(("exp", "enc"), None),
        P(("exp", "enc"), None),
        P(),
        P("exp", None, "seq"),
        P("exp", None, "seq"),
        P("exp", "seq", None),
    )
    out_specs = (P(("exp", "enc"), "seq"), P("exp", "enc"))
    body = functools.partial(shards, dict(mesh.shape))
    return jax.shard_map(body, mesh=mesh, in_specs=in_specs, out_specs=out_specs, check_vma=False)
```

```python
import functools

import jax
import jax.numpy as jnp
from jax import lax
from jax.experimental import pallas as pl
from jax.experimental.pallas import tpu as pltpu
from jax.sharding import PartitionSpec as P

MERGE = 4
CAP = 3
PIECE = 4
GROUP = 8
BF = jnp.bfloat16
F32 = jnp.float32
I32 = jnp.int32
MESH = pl.DeviceIdType.MESH


def up(value, step):
    return -(-value // step) * step


def iota(shape, axis):
    return lax.broadcasted_iota(I32, shape, axis)


def mm(a, b):
    return jnp.dot(a, b, preferred_element_type=F32)


def kernel(
    dims,
    counts_ref, order_ref, patches_ref, wm_hbm, w2_hbm, routes_ref, weight_ref, place_ref,
    wg_hbm, wu_hbm, wd_hbm,
    out_ref, load_ref,
    raw, nb, wm, w2, wg, wu, wd, acc1, ib, place_mat, acc2, psend, precv, xbuf,
    slot_send, rs, lf, dsend, drecv, ysend, yrecv, mix, gsel, gcnt,
    raw_sem, wm_sem, w2_sem, wx_sem,
    ny_s, ny_r, nc_s, nc_r, ib_s, ib_r, ps_s, ps_r, sl_s, sl_r, fw_s, fw_r, dn_s, dn_r, bk_s, bk_r,
    own_sem,
):
    ns, ne, nc_enc, cap_img, rp, wr, vit, units, cols, chunk, tok, top, n_all, hid = dims
    nchunk = cols // chunk
    s, e, c = lax.axis_index("seq"), lax.axis_index("exp"), lax.axis_index("enc")
    other = lax.rem(c + 1, nc_enc)

    def to_seq(j):
        return {"seq": lax.rem(s + j, ns)}

    def from_seq(j):
        return lax.rem(s + ns - j, ns)

    core = {"enc": other}

    def to_exp(k):
        return {"exp": lax.rem(e + k, ne)}

    def remote(src, dst, send, recv, dev):
        return pltpu.make_async_remote_copy(
            src_ref=src, dst_ref=dst, send_sem=send, recv_sem=recv, device_id=dev,
            device_id_type=MESH,
        )

    raw_copy = pltpu.make_async_copy(patches_ref.at[0, 0], raw, raw_sem)
    raw_copy.start()
    wm_copies = [
        pltpu.make_async_copy(
            wm_hbm.at[:, pl.ds(m * vit, vit)], wm.at[m], wm_sem.at[m]
        )
        for m in range(MERGE)
    ]
    for cp in wm_copies:
        cp.start()
    w2_copies = []
    for j in range(ns):
        b = from_seq(j)
        w2_copies.append(pltpu.make_async_copy(w2_hbm.at[b, 0], w2.at[b], w2_sem.at[j]))
    for cp in w2_copies:
        cp.start()
    wx_copies = [
        pltpu.make_async_copy(wg_hbm.at[0], wg, wx_sem.at[0]),
        pltpu.make_async_copy(wu_hbm.at[0], wu, wx_sem.at[1]),
        pltpu.make_async_copy(wd_hbm.at[0], wd, wx_sem.at[2]),
    ]
    for cp in wx_copies:
        cp.start()

    ib[...] = jnp.zeros(ib.shape, BF)
    barrier = pltpu.get_barrier_semaphore()
    for j in range(1, ns):
        pl.semaphore_signal(barrier, inc=1, device_id=to_seq(j), device_id_type=MESH)
    pl.semaphore_signal(barrier, inc=1, device_id=core, device_id_type=MESH)
    for k in range(1, ne):
        pl.semaphore_signal(barrier, inc=1, device_id=to_exp(k), device_id_type=MESH)

    raw_copy.wait()
    values = raw[...].astype(F32)
    centred = values - jnp.mean(values, axis=1, keepdims=True)
    variance = jnp.mean(centred * centred, axis=1, keepdims=True)
    normed = (centred * lax.rsqrt(variance + 1e-06)).astype(BF)
    rows_in = cap_img * MERGE
    k_i, r_i = iota((rp, rows_in), 0), iota((rp, rows_in), 1)
    def nb_at(p, cc, m):
        return nb.at[p, cc, m, pl.ds(0, wr)]

    pending = []
    pl.semaphore_wait(barrier, ns - 1 + 1 + ne - 1)
    for m in range(MERGE):
        pick = jnp.where((k_i < cap_img) & (r_i == k_i * MERGE + m), 1.0, 0.0).astype(BF)
        nb[s, c, m] = mm(pick, normed).astype(BF)
        for j in range(1, ns):
            cp = remote(nb_at(s, c, m), nb_at(s, c, m), ny_s.at[j, m], ny_r.at[j, m], to_seq(j))
            cp.start()
            pending.append(cp)
        cp = remote(nb_at(s, c, m), nb_at(s, c, m), nc_s.at[0, m], nc_r.at[0, m], core)
        cp.start()
        pending.append(cp)

    live = lax.rem(iota((nc_enc * rp, 1), 0), rp) < cap_img

    def ib_at(b, p):
        return ib.at[b, p, :, pl.ds(0, wr)]

    def finish_inner(p):
        a = acc1[...]
        inner = 0.5 * a * (1.0 + lax.erf(a * 0.7071067811865476))
        ib[s, p] = jnp.where(live, inner, 0.0).astype(BF).reshape(nc_enc, rp, units)

    def send_inner(p, j0):
        for j in range(1, ns):
            cp = remote(ib_at(s, p), ib_at(s, p), ib_s.at[j, j0], ib_r.at[j, j0], to_seq(j))
            cp.start()
            pending.append(cp)

    def mm1(p, m):
        lhs = nb[p, :, m].reshape(nc_enc * rp, vit)
        term = lax.dot_general(
            lhs, wm[m], (((1,), (1,)), ((), ())), preferred_element_type=F32
        )
        if m == 0:
            acc1[...] = term
        else:
            acc1[...] += term

    ncol = mix.shape[1] // 3
    place = place_ref[...].reshape(1, n_all)
    d_of = iota((ncol, n_all), 0) // GROUP
    number = iota((ncol, n_all), 1)
    expert = jnp.sum(jnp.where(place == d_of, number, 0), axis=1, keepdims=True)
    row = iota((ncol, 1), 0)
    expert = jnp.where(row < ne * GROUP, expert, -1)
    q_of = lax.rem(row, GROUP)
    named = jnp.zeros((ncol, tok), F32)
    amount = jnp.zeros((ncol, tok), F32)
    for k in range(top):
        match = routes_ref[k : k + 1, :] == expert
        named = jnp.where(match, 1.0, named)
        amount = amount + jnp.where(match, weight_ref[k : k + 1, :], 0.0)
    earlier = jnp.where(iota((tok, tok), 0) < iota((tok, tok), 1), 1.0, 0.0).astype(BF)
    rank = mm(named.astype(BF), earlier)
    chosen = jnp.where((rank == q_of.astype(F32)) & (q_of < CAP), named, 0.0)
    mixing = jnp.transpose(chosen * amount)
    part_a = mixing.astype(BF)
    rest = mixing - part_a.astype(F32)
    part_b = rest.astype(BF)
    part_c = (rest - part_b.astype(F32)).astype(BF)
    mix[:, 0:ncol] = part_a
    mix[:, ncol : 2 * ncol] = part_b
    mix[:, 2 * ncol : 3 * ncol] = part_c
    gsel[...] = chosen.astype(BF)
    counted = jnp.where(q_of == CAP, named, 0.0)
    gcnt[...] = jnp.broadcast_to(jnp.sum(counted, axis=1, keepdims=True), gcnt.shape)
    lf[...] = jnp.zeros(lf.shape, F32)

    shard_total = ns * nc_enc
    starts, run = [], jnp.int32(0)
    for i in range(shard_total):
        starts.append(run)
        o_i = order_ref[0, i]
        for j in range(shard_total):
            run = run + jnp.where(o_i == j, counts_ref[0, j], 0)
    seq_len = tok * nc_enc
    position = lax.rem(iota((seq_len, rp), 0) + other * tok, seq_len)
    k_row = iota((seq_len, rp), 1)
    for j in range(shard_total):
        first = jnp.int32(0)
        for i in range(shard_total):
            first = first + jnp.where(order_ref[0, i] == j, starts[i], 0)
        hit = (position - first == k_row) & (k_row < counts_ref[0, j])
        place_mat[j] = jnp.where(hit, 1.0, 0.0).astype(BF)

    for m in range(MERGE):
        wm_copies[m].wait()
        remote(
            nb_at(s, other, m), nb_at(s, other, m), nc_s.at[0, m], nc_r.at[0, m], core
        ).wait_recv()
        mm1(s, m)
    finish_inner(s)
    send_inner(s, 0)
    for j in range(1, ns):
        p = from_seq(j)
        for m in range(MERGE):
            remote(
                nb_at(p, c, m), nb_at(p, c, m), ny_s.at[j, m], ny_r.at[j, m], to_seq(j)
            ).wait_recv()
            cp = remote(nb_at(p, c, m), nb_at(p, c, m), nc_s.at[j, m], nc_r.at[j, m], core)
            cp.start()
            pending.append(cp)
            remote(
                nb_at(p, other, m), nb_at(p, other, m), nc_s.at[j, m], nc_r.at[j, m], core
            ).wait_recv()
            mm1(p, m)
        finish_inner(p)
        send_inner(p, j)

    def placed_of(b):
        total = jnp.zeros((seq_len, units), F32)
        for p in range(ns):
            for cc in range(nc_enc):
                total += mm(place_mat[p * nc_enc + cc], ib[b, p, cc])
        return total.astype(BF)

    def columns_at(n):
        return pl.ds(pl.multiple_of(n * chunk, chunk), chunk)

    for j in range(ns):
        b = from_seq(j)
        if j > 0:
            for t in range(ns):
                src_p = lax.rem(b + ns - t, ns)
                remote(
                    ib_at(b, src_p), ib_at(b, src_p), ib_s.at[j, t], ib_r.at[j, t], to_seq(j)
                ).wait_recv()
        w2_copies[j].wait()
        placed = placed_of(b)
        for n in range(nchunk):
            term = mm(placed, w2[b, :, n * chunk : (n + 1) * chunk])
            if j > 0:
                term = acc2[n] + term
            if j < ns - 1:
                acc2[n] = term
            else:
                psend[n] = term[0:tok].astype(BF)
                xbuf[n] = term[tok : 2 * tok].astype(BF)
                cp = remote(psend.at[n], precv.at[n], ps_s.at[n], ps_r.at[n], core)
                cp.start()
                pending.append(cp)

    flag_row = lax.rem(iota((ncol, 1), 0), GROUP) == CAP
    for n in range(nchunk):
        remote(psend.at[n], precv.at[n], ps_s.at[n], ps_r.at[n], core).wait_recv()
        x = (xbuf[n].astype(F32) + precv[n].astype(F32)).astype(BF)
        xbuf[n] = x
        rows = jnp.where(flag_row, gcnt[:, 0:1], mm(gsel[...], x))
        for d in range(ne):
            slot_send[d, :, n * chunk : (n + 1) * chunk] = rows[
                d * GROUP : d * GROUP + PIECE
            ].astype(BF)

    for k in range(1, ne):
        dst = lax.rem(e + k, ne)
        cp = remote(slot_send.at[dst], rs.at[s, e], sl_s.at[k], sl_r.at[k], to_exp(k))
        cp.start()
        pending.append(cp)
    own_copy = pltpu.make_async_copy(slot_send.at[e], rs.at[s, e], own_sem.at[0])
    own_copy.start()
    for k in range(ne):
        src = lax.rem(e + ne - k, ne)
        if k == 0:
            own_copy.wait()
        else:
            remote(slot_send.at[e], rs.at[s, src], sl_s.at[k], sl_r.at[k], to_exp(k)).wait_recv()
        for j in range(1, ns):
            cp = remote(rs.at[s, src], rs.at[s, src], fw_s.at[j, k], fw_r.at[j, k], to_seq(j))
            cp.start()
            pending.append(cp)

    rows_e = ne * GROUP
    gate_sum = jnp.zeros((rows_e, hid), F32)
    up_sum = jnp.zeros((rows_e, hid), F32)
    squares = jnp.zeros((rows_e, 1), F32)
    wx_copies[0].wait()
    wx_copies[1].wait()
    for j in range(ns):
        p = from_seq(j)
        if j > 0:
            for k in range(ne):
                src = lax.rem(e + ne - k, ne)
                remote(
                    rs.at[p, src], rs.at[p, src], fw_s.at[j, k], fw_r.at[j, k], to_seq(j)
                ).wait_recv()
        for d in range(ne):
            lf[d * GROUP : d * GROUP + PIECE] = rs[p, d].astype(F32)
        if j == 0:
            tile = lf[:, 0:128]
            flagged = (lax.rem(iota(tile.shape, 0), GROUP) == CAP) & (iota(tile.shape, 1) == 0)
            filled = jnp.where(flagged, tile, 0.0)
            filled = jnp.sum(jnp.sum(filled, axis=1, keepdims=True), axis=0, keepdims=True)
            load_ref[...] = filled * (n_all / (ne * tok * top))
        for n in range(nchunk):
            block = lf[:, n * chunk : (n + 1) * chunk]
            squares = squares + jnp.sum(block * block, axis=1, keepdims=True)
            lhs = block.astype(BF)
            at = pl.ds(pl.multiple_of(p * cols + n * chunk, chunk), chunk)
            gate_sum = gate_sum + mm(lhs, wg[at, :])
            up_sum = up_sum + mm(lhs, wu[at, :])
    inv_rms = lax.rsqrt(squares / (ns * cols) + 1e-06)
    gate = gate_sum * inv_rms
    hidden = (gate / (1.0 + jnp.exp(-gate)) * (up_sum * inv_rms)).astype(BF)
    wx_copies[2].wait()

    def down_copy(j, n):
        at = pl.ds(n * chunk, chunk)
        return remote(
            dsend.at[j, :, :, at], drecv.at[j, :, :, at], dn_s.at[j, n], dn_r.at[j, n], to_seq(j)
        )

    for j in list(range(1, ns)) + [0]:
        p = lax.rem(s + j, ns)
        for n in range(nchunk):
            at = pl.ds(pl.multiple_of(p * cols + n * chunk, chunk), chunk)
            term = mm(hidden, wd[:, at])
            for d in range(ne):
                dsend[j, d, :, n * chunk : (n + 1) * chunk] = term[
                    d * GROUP : d * GROUP + PIECE
                ].astype(BF)
            if j > 0:
                cp = down_copy(j, n)
                cp.start()
                pending.append(cp)
    for n in range(nchunk):
        at = pl.ds(n * chunk, chunk)
        total = dsend[0, :, :, at].astype(F32)
        for j in range(1, ns):
            down_copy(j, n).wait_recv()
            total = total + drecv[j, :, :, at].astype(F32)
        ysend[:, :, at] = total.astype(BF)
    for k in range(1, ne):
        dst = lax.rem(e + k, ne)
        cp = remote(ysend.at[dst], yrecv.at[e], bk_s.at[k], bk_r.at[k], to_exp(k))
        cp.start()
        pending.append(cp)
    back_copy = pltpu.make_async_copy(ysend.at[e], yrecv.at[e], own_sem.at[1])
    back_copy.start()
    back_copy.wait()
    for k in range(1, ne):
        src = lax.rem(e + ne - k, ne)
        remote(ysend.at[e], yrecv.at[src], bk_s.at[k], bk_r.at[k], to_exp(k)).wait_recv()
    for d in range(ne):
        lf[d * GROUP : d * GROUP + PIECE] = yrecv[d].astype(F32)
    for n in range(nchunk):
        y = lf[:, n * chunk : (n + 1) * chunk].astype(BF)
        if ncol > rows_e:
            y = jnp.concatenate([y, jnp.zeros((ncol - rows_e, chunk), BF)], axis=0)
        combined = mm(mix[...], jnp.concatenate([y, y, y], axis=0))
        out_ref[:, n * chunk : (n + 1) * chunk] = (xbuf[n].astype(F32) + combined).astype(BF)
    for cp in pending:
        cp.wait_send()


def shards(mesh_shape, *args):
    (patches, image_counts, image_order, w_merge, w_proj_out, routes, route_weight,
     expert_place, w_gate, w_up, w_down) = args
    ns, ne, nc = mesh_shape["seq"], mesh_shape["exp"], mesh_shape["enc"]
    rows_in, vit = patches.shape[2:]
    cap_img = rows_in // MERGE
    rp = up(cap_img, 16)
    wr = up(cap_img, 8)
    units = w_merge.shape[1]
    cols = w_proj_out.shape[3]
    tok, top = routes.shape
    n_all = expert_place.shape[0]
    hid = w_gate.shape[2]
    chunk = [w for w in (512, 256, 128) if cols % w == 0][0]
    nchunk = cols // chunk
    ncol = up(ne * GROUP, 128)
    dims = (ns, ne, nc, cap_img, rp, wr, vit, units, cols, chunk, tok, top, n_all, hid)
    anyspec = pl.BlockSpec(memory_space=pl.ANY)
    vmem = pl.BlockSpec(memory_space=pltpu.VMEM)
    smem = pl.BlockSpec(memory_space=pltpu.SMEM)
    dma = pltpu.SemaphoreType.DMA
    V = pltpu.VMEM
    scratch = [
        V((rows_in, vit), BF),
        V((ns, nc, MERGE, rp, vit), BF),
        V((MERGE, units, vit), BF),
        V((ns, units, cols), BF),
        V((ns * cols, hid), BF),
        V((ns * cols, hid), BF),
        V((hid, ns * cols), BF),
        V((nc * rp, units), F32),
        V((ns, ns, nc, rp, units), BF),
        V((ns * nc, tok * nc, rp), BF),
        V((nchunk, tok * nc, chunk), F32),
        V((nchunk, tok, chunk), BF),
        V((nchunk, tok, chunk), BF),
        V((nchunk, tok, chunk), BF),
        V((ne, PIECE, cols), BF),
        V((ns, ne, PIECE, cols), BF),
        V((ne * GROUP, cols), F32),
        V((ns, ne, PIECE, cols), BF),
        V((ns, ne, PIECE, cols), BF),
        V((ne, PIECE, cols), BF),
        V((ne, PIECE, cols), BF),
        V((tok, 3 * ncol), BF),
        V((ncol, tok), BF),
        V((ncol, 128), F32),
        dma, dma((MERGE,)), dma((ns,)), dma((3,)),
        dma((ns, MERGE)), dma((ns, MERGE)), dma((ns, MERGE)), dma((ns, MERGE)),
        dma((ns, ns)), dma((ns, ns)), dma((nchunk,)), dma((nchunk,)),
        dma((ne,)), dma((ne,)), dma((ns, ne)), dma((ns, ne)),
        dma((ns, nchunk)), dma((ns, nchunk)), dma((ne,)), dma((ne,)),
        dma((2,)),
    ]
    return pl.pallas_call(
        functools.partial(kernel, dims),
        out_shape=(
            jax.ShapeDtypeStruct((tok, cols), BF),
            jax.ShapeDtypeStruct((1, 1), F32),
        ),
        in_specs=[smem, smem, anyspec, anyspec, anyspec, vmem, vmem, vmem] + [anyspec] * 3,
        out_specs=(vmem, vmem),
        scratch_shapes=scratch,
        compiler_params=pltpu.CompilerParams(
            collective_id=0, has_side_effects=True, vmem_limit_bytes=67043328
        ),
        name="step",
    )(
        image_counts, image_order, patches, w_merge.T, w_proj_out, routes.T, route_weight.T,
        expert_place, w_gate, w_up, w_down,
    )


def solution(mesh):
    in_specs = (
        P("exp", ("seq", "enc"), None, None),
        P("exp", None),
        P("exp", None),
        P(None, ("seq", "enc")),
        P(None, "enc", None, "seq"),
        P(("exp", "enc"), None),
        P(("exp", "enc"), None),
        P(),
        P("exp", None, "seq"),
        P("exp", None, "seq"),
        P("exp", "seq", None),
    )
    out_specs = (P(("exp", "enc"), "seq"), P("exp", "enc"))
    body = functools.partial(shards, dict(mesh.shape))
    return jax.shard_map(body, mesh=mesh, in_specs=in_specs, out_specs=out_specs, check_vma=False)
```
